32 devices in a mesh: grp: 2 (over y), row: 4 (over z), col: 2 (over x), frm: 2 (over core).
Axes of the slice: x: 2, y: 2, z: 4, core: 2. Of those that a mesh axis runs over, the one named last changes fastest.
Arguments:
- latent: bfloat16 [4, 16, 320, 256], P(('grp', 'frm'), 'row', 'col'), parts along dimension 0, may hold values from -6 to 6
- proj_weight: bfloat16 [256, 128], replicated, may hold values from -0.375 to 0.375
- proj_bias: float32 [128], replicated, may hold values from -3 to 3
- cache_one: bfloat16 [4, 32, 640, 128], P(('grp', 'frm'), 'row', 'col'), parts along dimension 0, may hold values from -6 to 6
- cache_two: bfloat16 [4, 32, 640, 128], P(('grp', 'frm'), 'row', 'col'), parts along dimension 0, may hold values from -6 to 6
- conv_one: bfloat16 [3, 3, 3, 128, 128], replicated, may hold values from -0.109375 to 0.109375
- bias_one: float32 [128], replicated, may hold values from -3 to 3
- conv_two: bfloat16 [3, 3, 3, 128, 128], replicated, may hold values from -0.109375 to 0.109375
- bias_two: float32 [128], replicated, may hold values from -3 to 3
Outputs:
- decoded: bfloat16 [4, 32, 640, 128], P(('grp', 'frm'), 'row', 'col'), parts along dimension 0
The draws below stay inside these ranges and needn't reach their ends.
There are 2 independent parts, one for each index of `grp`. The reference program is written for one: setup_inputs(seed, part) draws one part's arguments, and reference() takes and returns one part's arrays. A program takes and returns all parts, laid end to end along the dimension named above; an argument that names none is the same for every part. Nothing has to cross between parts.
All inputs are finite; a program needn't handle non-finite values.
Results may differ from the reference program's by a relative error of at most 0.0044.
Values may be sent and summed in bfloat16 or wider, within the bound.
A program may use at most 64 MiB of HBM per device.

```python
import jax
import jax.numpy as jnp

LCH = 256
CH = 128
FRAMES = 2
H = 32
W = 640
LH = 16
LW = 320


def block_scale(rng, extent, shards, least, top_value):
    loudness = 1.0
    for dim, parts in shards:
        steps = jax.random.uniform(jax.random.fold_in(jax.random.fold_in(rng, 6), dim), (parts,), jnp.float32, least / len(shards), top_value / len(shards))
        loudness = loudness * jnp.repeat(jnp.exp(steps), extent[dim] // parts).reshape((-1,) + (1,) * (len(extent) - 1 - dim))
    return loudness


def centred(rng, dims, scale, limit, split=(), dtype=jnp.bfloat16):
    gain = block_scale(rng, dims, split, -0.22, 0.18) if split else 1.0
    values = jax.random.normal(rng, dims, jnp.float32) * scale * gain
    return jnp.minimum(jnp.maximum(values, -limit), limit).astype(dtype)


def setup_inputs(seed: int = 0, part: int = 0) -> dict:
    keys = jax.random.split(jax.random.key(seed), 10)
    own_keys = jax.random.split(jax.random.fold_in(keys[9], part), 10)
    latent = centred(own_keys[0], (FRAMES, LH, LW, LCH), 1.0, 6.0, ((0, 2), (1, 4), (2, 2)))
    proj_weight = centred(keys[1], (LCH, CH), LCH ** -0.5, 0.375)
    proj_bias = centred(keys[2], (CH,), 0.5, 3.0, (), jnp.float32)
    cache_one = centred(own_keys[3], (FRAMES, H, W, CH), 1.0, 6.0, ((0, 2), (1, 4), (2, 2)))
    cache_two = centred(own_keys[4], (FRAMES, H, W, CH), 1.0, 6.0, ((0, 2), (1, 4), (2, 2)))
    conv_one = centred(keys[5], (3, 3, 3, CH, CH), (27 * CH) ** -0.5, 0.109375)
    bias_one = centred(keys[6], (CH,), 0.5, 3.0, (), jnp.float32)
    conv_two = centred(keys[7], (3, 3, 3, CH, CH), (27 * CH) ** -0.5, 0.109375)
    bias_two = centred(keys[8], (CH,), 0.5, 3.0, (), jnp.float32)
    return {"latent": latent, "proj_weight": proj_weight, "proj_bias": proj_bias, "cache_one": cache_one, "cache_two": cache_two, "conv_one": conv_one, "bias_one": bias_one, "conv_two": conv_two, "bias_two": bias_two}


def causal_conv(frames, weight, bias):
    tile_rows, tile_cols, channels = frames.shape[1], frames.shape[2], frames.shape[3]
    padded = jnp.pad(frames, ((0, 0), (1, 1), (1, 1), (0, 0)))
    folded = weight.reshape(3, 3, 3 * channels, weight.shape[-1])
    results = []
    for frame_out in range(frames.shape[0] - 2):
        summed = jnp.zeros((tile_rows * tile_cols, weight.shape[-1]), jnp.float32)
        for frame_step in range(3):
            for row_step in range(3):
                stencil = jnp.concatenate(
                    [padded[frame_out + frame_step, row_step:row_step + tile_rows, col_step:col_step + tile_cols]
                     for col_step in range(3)], axis=-1).reshape(tile_rows * tile_cols, 3 * channels)
                summed = summed + jnp.dot(stencil, folded[frame_step, row_step], preferred_element_type=jnp.float32)
        results.append((summed + bias).reshape(tile_rows, tile_cols, -1))
    return jnp.stack(results)


def reference(latent, proj_weight, proj_bias, cache_one, cache_two, conv_one, bias_one, conv_two, bias_two):
    projected = jnp.dot(latent.reshape(-1, latent.shape[-1]), proj_weight, preferred_element_type=jnp.float32) + proj_bias
    projected = projected.reshape(latent.shape[0], latent.shape[1], latent.shape[2], -1)
    upsampled = jnp.repeat(jnp.repeat(projected.astype(jnp.bfloat16), 2, axis=1), 2, axis=2)
    act_one = jax.nn.silu(upsampled.astype(jnp.float32)).astype(jnp.bfloat16)
    first_out = causal_conv(jnp.concatenate([cache_one, act_one], axis=0), conv_one, bias_one)
    act_two = jax.nn.silu(first_out).astype(jnp.bfloat16)
    second_out = causal_conv(jnp.concatenate([cache_two, act_two], axis=0), conv_two, bias_two)
    return (upsampled.astype(jnp.float32) + second_out).astype(jnp.bfloat16)
```

```python
import functools

import jax
import jax.numpy as jnp
from jax import lax
from jax.experimental import pallas as pl
from jax.experimental.pallas import tpu as pltpu
from jax.sharding import PartitionSpec as P

EDGE = 16
STEP = 2
MESH = pl.DeviceIdType.MESH
SIDES = [(-1, 0), (1, 0), (0, -1), (0, 1), (-1, -1), (-1, 1), (1, -1), (1, 1)]


def kernel(rows_n, cols_n, lat_h, pw_h, pb, c1_h, c2_h, w1_h, b1, w2_h, b2, out_h,
           lat, pw, w, F, L, up, obuf, s1, s2,
           load_sem, send_sem, recv_sem, mid_send, mid_recv, out_sem):
    R, W = c1_h.shape[1], c1_h.shape[2]
    CH = c1_h.shape[3]
    WP = W + EDGE
    HR, HW = lat.shape[0], lat.shape[1]
    blocks = R // STEP
    r, c, f = lax.axis_index("row"), lax.axis_index("col"), lax.axis_index("frm")
    caches = (c1_h, c2_h)
    up_ok, down_ok = r > 0, r < rows_n - 1
    left_ok, right_ok = c > 0, c < cols_n - 1

    def exists(d):
        dr, dc = SIDES[d]
        ok = None
        for test in ([up_ok] if dr < 0 else [down_ok] if dr > 0 else []) + (
                [left_ok] if dc < 0 else [right_ok] if dc > 0 else []):
            ok = test if ok is None else jnp.logical_and(ok, test)
        return ok

    def where_is(d):
        dr, dc = SIDES[d]
        ids = {}
        if dr:
            ids["row"] = r + dr
        if dc:
            ids["col"] = c + dc
        return ids

    loads = []

    def load(src, dst):
        cp = pltpu.make_async_copy(src, dst, load_sem.at[len(loads)])
        cp.start()
        loads.append(cp)
        return cp

    lat_cp = load(lat_h.at[0], lat)
    pw_cp = load(pw_h, pw)
    cache_cp = [load(caches[0].at[0], F.at[0, 0, pl.ds(1, R), pl.ds(0, W)])]
    w_cp = [[load(w1_h.at[:, :, q], w.at[0, :, :, :, pl.ds(q * CH, CH)]) for q in range(3)]]
    cache_cp.append(load(caches[1].at[0], F.at[1, 0, pl.ds(1, R), pl.ds(0, W)]))
    w_cp.append([load(w2_h.at[:, :, q], w.at[1, :, :, :, pl.ds(q * CH, CH)]) for q in range(3)])

    barrier = pltpu.get_barrier_semaphore()
    for d in range(8):
        @pl.when(exists(d))
        def _():
            pl.semaphore_signal(barrier, inc=1, device_id=where_is(d), device_id_type=MESH)
    pl.semaphore_signal(barrier, inc=1, device_id={"frm": 1 - f}, device_id_type=MESH)
    tall = 1 + up_ok.astype(jnp.int32) + down_ok.astype(jnp.int32)
    wide = 1 + left_ok.astype(jnp.int32) + right_ok.astype(jnp.int32)
    pl.semaphore_wait(barrier, tall * wide)

    def side_copy(cv, which, d, from_hbm=False):
        dr, dc = SIDES[d]
        row = 0 if dr < 0 else R - 1
        land_row = R + 1 if dr < 0 else 0
        col = pl.ds(0, EDGE) if dc < 0 else pl.ds(W - EDGE, EDGE)
        side = 1 if dc < 0 else 0
        fr = 2 * which
        if dc == 0:
            rs, cs = pl.ds(row, 1), pl.ds(0, W)
            dst = F.at[cv, fr, pl.ds(land_row, 1), pl.ds(0, W)]
        elif dr == 0:
            rs, cs = pl.ds(0, R), col
            dst = L.at[cv, which, side, pl.ds(1, R)]
        else:
            rs, cs = pl.ds(row, 1), col
            dst = L.at[cv, which, side, pl.ds(land_row, 1)]
        if from_hbm:
            src = caches[cv].at[0, rs, cs]
        else:
            src = F.at[cv, fr, pl.ds(1 + rs.start, rs.size), cs]
        return pltpu.make_async_remote_copy(
            src_ref=src, dst_ref=dst, send_sem=send_sem.at[cv, which, d],
            recv_sem=recv_sem.at[cv, which, d], device_id=where_is(d), device_id_type=MESH)

    def send_sides(cv, which, ds, from_hbm=False):
        for d in ds:
            @pl.when(exists(d))
            def _():
                side_copy(cv, which, d, from_hbm).start()

    def recv_sides(cv, which, ds):
        for d in ds:
            opposite = SIDES.index((-SIDES[d][0], -SIDES[d][1]))

            @pl.when(exists(opposite))
            def _():
                side_copy(cv, which, d, which == 0).wait_recv()

    def drain_sides(cv, which):
        for d in range(8):
            @pl.when(exists(d))
            def _():
                side_copy(cv, which, d, which == 0).wait_send()

    partner = {"frm": 1 - f}

    def main_copy(cv, i, cache):
        here = pl.ds(1 + i * STEP, STEP)
        if cache:
            src = caches[cv].at[0, pl.ds(i * STEP, STEP)]
        else:
            src = F.at[cv, 2, here, pl.ds(0, W)]
        return pltpu.make_async_remote_copy(
            src_ref=src, dst_ref=F.at[cv, 1, here, pl.ds(0, W)], send_sem=mid_send.at[cv, i],
            recv_sem=mid_recv.at[cv, i], device_id=partner, device_id_type=MESH)

    payload = 2 * (1 - f)

    def rim_copy(cv, part):
        if part < 2:
            rs, cs = pl.ds((R + 1) * part, 1), pl.ds(0, WP)
        else:
            rs, cs = pl.ds(1, R), pl.ds(W, EDGE)
        return pltpu.make_async_remote_copy(
            src_ref=F.at[cv, payload, rs, cs], dst_ref=F.at[cv, 1, rs, cs],
            send_sem=mid_send.at[cv, blocks + part], recv_sem=mid_recv.at[cv, blocks + part],
            device_id=partner, device_id_type=MESH)

    def merge(cv, which):
        left, right = L[cv, which, 0], L[cv, which, 1]
        place = lax.broadcasted_iota(jnp.int32, left.shape, 1)
        tile = jnp.where(place < EDGE // 2, right.astype(jnp.float32), left.astype(jnp.float32))
        F[cv, 2 * which, :, pl.ds(W, EDGE)] = tile.astype(jnp.bfloat16)

    send_sides(0, 0, range(8), True)

    @pl.when(f == 1)
    def _():
        for i in range(blocks):
            main_copy(0, i, True).start()

    for cv in range(2):
        for which in range(2):
            for ok, row in ((up_ok, 0), (down_ok, R + 1)):
                @pl.when(jnp.logical_not(ok))
                def _():
                    F[cv, 2 * which, row, pl.ds(0, W)] = jnp.zeros((W, CH), jnp.bfloat16)

                for side, across in ((0, left_ok), (1, right_ok)):
                    @pl.when(jnp.logical_not(jnp.logical_and(ok, across)))
                    def _():
                        L[cv, which, side, row] = jnp.zeros((EDGE, CH), jnp.bfloat16)
            for side, across in ((0, left_ok), (1, right_ok)):
                @pl.when(jnp.logical_not(across))
                def _():
                    L[cv, which, side, pl.ds(1, R)] = jnp.zeros((R, EDGE, CH), jnp.bfloat16)

    lat_cp.wait()
    pw_cp.wait()

    def project(i, carry):
        v = jnp.dot(lat[i], pw[...], preferred_element_type=jnp.float32) + pb[...]
        v = v.astype(jnp.bfloat16).astype(jnp.float32)
        a = v / (1.0 + jnp.exp(-v))
        for k in range(2):
            s1[pl.ds(k, HW, stride=2), :] = v
            s2[pl.ds(k, HW, stride=2), :] = a
        up[i] = s1[...].astype(jnp.bfloat16)
        wide = s2[...].astype(jnp.bfloat16)
        F[0, 2, 1 + 2 * i, pl.ds(0, W)] = wide
        F[0, 2, 2 + 2 * i, pl.ds(0, W)] = wide
        return carry

    lax.fori_loop(0, HR, project, 0)
    send_sides(0, 1, range(8))

    @pl.when(f == 0)
    def _():
        for i in range(blocks):
            main_copy(0, i, False).start()

    send_sides(1, 0, range(8), True)

    @pl.when(f == 1)
    def _():
        for i in range(blocks):
            main_copy(1, i, True).start()

    def taps(cv, first, count, base):
        lhs = jnp.concatenate(
            [F[cv, a, pl.ds(base + p, STEP)].reshape(STEP * WP, CH)
             for a in range(first, first + count) for p in range(3)], axis=1)
        rhs = w[cv, pl.ds(first, count)].reshape(count * 3 * CH, 3 * CH)
        return jnp.dot(lhs, rhs, preferred_element_type=jnp.float32)

    def fold(z, n):
        z = z[n * WP:(n + 1) * WP]
        return (pltpu.roll(z[:, :CH], 1, 0)[:W] + z[:W, CH:2 * CH]
                + pltpu.roll(z[:, 2 * CH:], WP - 1, 0)[:W])

    def arrive(cv):
        recv_sides(cv, 0, range(8))
        merge(cv, 0)
        recv_sides(cv, 1, range(8))
        merge(cv, 1)
        for part in range(3):
            rim_copy(cv, part).start()
        for i in range(blocks):
            main_copy(cv, i, False).wait_recv()
        for part in range(3):
            rim_copy(cv, part).wait_recv()

    cache_cp[0].wait()
    for cp in w_cp[0]:
        cp.wait()
    arrive(0)

    def first(k, carry):
        i = lax.rem(k + blocks - 1, blocks)
        base = i * STEP
        z = taps(0, 0, 3, base)
        for n in range(STEP):
            y = fold(z, n) + b1[...]
            F[1, 2, base + n + 1, pl.ds(0, W)] = (y / (1.0 + jnp.exp(-y))).astype(jnp.bfloat16)

        @pl.when(k == 1)
        def _():
            send_sides(1, 1, (0, 1, 4, 5, 6, 7))

        @pl.when(f == 0)
        def _():
            main_copy(1, i, False).start()
        return carry

    lax.fori_loop(0, blocks, first, 0)
    send_sides(1, 1, (2, 3))
    cache_cp[1].wait()
    for cp in w_cp[1]:
        cp.wait()
    arrive(1)

    def second(k, carry):
        i = lax.rem(k + 1, blocks)
        base = i * STEP
        z = taps(1, 0, 3, base)
        for n in range(STEP):
            y = fold(z, n) + b2[...] + up[(base + n) // 2].astype(jnp.float32)
            obuf[base + n] = y.astype(jnp.bfloat16)
        pltpu.make_async_copy(obuf.at[pl.ds(base, STEP)], out_h.at[0, pl.ds(base, STEP)],
                              out_sem.at[i]).start()
        return carry

    lax.fori_loop(0, blocks, second, 0)
    for cv in range(2):
        for which in range(2):
            drain_sides(cv, which)
        for i in range(blocks):
            main_copy(cv, i, False).wait_send()
        for part in range(3):
            rim_copy(cv, part).wait_send()
    for i in range(blocks):
        pltpu.make_async_copy(obuf.at[pl.ds(i * STEP, STEP)], out_h.at[0, pl.ds(i * STEP, STEP)],
                              out_sem.at[i]).wait()


def per_device(latent, proj_weight, proj_bias, cache_one, cache_two,
               conv_one, bias_one, conv_two, bias_two):
    _, R, W, CH = cache_one.shape
    _, HR, HW, LCH = latent.shape
    blocks = R // STEP
    WP = W + EDGE
    anywhere = pl.BlockSpec(memory_space=pl.ANY)
    vmem = pl.BlockSpec(memory_space=pltpu.VMEM)
    bf = jnp.bfloat16
    return pl.pallas_call(
        functools.partial(kernel, lax.axis_size("row"), lax.axis_size("col")),
        out_shape=jax.ShapeDtypeStruct(cache_one.shape, bf),
        in_specs=[anywhere, anywhere, vmem, anywhere, anywhere, anywhere, vmem, anywhere, vmem],
        out_specs=anywhere,
        scratch_shapes=[
            pltpu.VMEM((HR, HW, LCH), bf),
            pltpu.VMEM((LCH, CH), bf),
            pltpu.VMEM((2, 3, 3, CH, 3 * CH), bf),
            pltpu.VMEM((2, 3, R + 2, WP, CH), bf),
            pltpu.VMEM((2, 2, 2, R + 2, EDGE, CH), bf),
            pltpu.VMEM((HR, W, CH), bf),
            pltpu.VMEM((R, W, CH), bf),
            pltpu.VMEM((W, CH), jnp.float32),
            pltpu.VMEM((W, CH), jnp.float32),
            pltpu.SemaphoreType.DMA((10,)),
            pltpu.SemaphoreType.DMA((2, 2, 8)),
            pltpu.SemaphoreType.DMA((2, 2, 8)),
            pltpu.SemaphoreType.DMA((2, blocks + 3)),
            pltpu.SemaphoreType.DMA((2, blocks + 3)),
            pltpu.SemaphoreType.DMA((blocks,)),
        ],
        compiler_params=pltpu.CompilerParams(
            collective_id=0, has_side_effects=True, vmem_limit_bytes=60 * 1024 * 1024),
        name="decoder_window",
    )(latent, proj_weight, proj_bias.reshape(1, CH), cache_one, cache_two,
      conv_one, bias_one.reshape(1, CH), conv_two, bias_two.reshape(1, CH))


def solution(mesh):
    placed = P(("grp", "frm"), "row", "col", None)
    return jax.shard_map(
        per_device,
        mesh=mesh,
        in_specs=(placed, P(), P(), placed, placed, P(), P(), P(), P()),
        out_specs=placed,
        check_vma=False,
    )
```

```python
import functools

import jax
import jax.numpy as jnp
from jax import lax
from jax.experimental import pallas as pl
from jax.experimental.pallas import tpu as pltpu
from jax.sharding import PartitionSpec as P

EDGE = 16
STEP = 2
MESH = pl.DeviceIdType.MESH
SIDES = [(-1, 0), (1, 0), (0, -1), (0, 1), (-1, -1), (-1, 1), (1, -1), (1, 1)]


def kernel(rows_n, cols_n, lat_h, pw_h, pb, c1_h, c2_h, w1_h, b1, w2_h, b2, out_h,
           lat, pw, w, F, L, up, obuf, acc, s1, s2,
           load_sem, send_sem, recv_sem, mid_send, mid_recv, out_sem):
    R, W = c1_h.shape[1], c1_h.shape[2]
    CH = c1_h.shape[3]
    WP = W + EDGE
    HR, HW = lat.shape[0], lat.shape[1]
    blocks = R // STEP
    r, c, f = lax.axis_index("row"), lax.axis_index("col"), lax.axis_index("frm")
    caches = (c1_h, c2_h)
    up_ok, down_ok = r > 0, r < rows_n - 1
    left_ok, right_ok = c > 0, c < cols_n - 1

    def exists(d):
        dr, dc = SIDES[d]
        ok = None
        for test in ([up_ok] if dr < 0 else [down_ok] if dr > 0 else []) + (
                [left_ok] if dc < 0 else [right_ok] if dc > 0 else []):
            ok = test if ok is None else jnp.logical_and(ok, test)
        return ok

    def where_is(d):
        dr, dc = SIDES[d]
        ids = {}
        if dr:
            ids["row"] = r + dr
        if dc:
            ids["col"] = c + dc
        return ids

    loads = []

    def load(src, dst):
        cp = pltpu.make_async_copy(src, dst, load_sem.at[len(loads)])
        cp.start()
        loads.append(cp)
        return cp

    lat_cp = load(lat_h.at[0], lat)
    pw_cp = load(pw_h, pw)
    cache_cp = [load(caches[0].at[0], F.at[0, 0, pl.ds(1, R), pl.ds(0, W)])]
    w_cp = [[load(w1_h.at[:, :, q], w.at[0, :, :, :, pl.ds(q * CH, CH)]) for q in range(3)]]
    cache_cp.append(load(caches[1].at[0], F.at[1, 0, pl.ds(1, R), pl.ds(0, W)]))
    w_cp.append([load(w2_h.at[:, :, q], w.at[1, :, :, :, pl.ds(q * CH, CH)]) for q in range(3)])

    barrier = pltpu.get_barrier_semaphore()
    for d in range(8):
        @pl.when(exists(d))
        def _():
            pl.semaphore_signal(barrier, inc=1, device_id=where_is(d), device_id_type=MESH)
    pl.semaphore_signal(barrier, inc=1, device_id={"frm": 1 - f}, device_id_type=MESH)
    tall = 1 + up_ok.astype(jnp.int32) + down_ok.astype(jnp.int32)
    wide = 1 + left_ok.astype(jnp.int32) + right_ok.astype(jnp.int32)
    pl.semaphore_wait(barrier, tall * wide)

    def side_copy(cv, which, d, from_hbm=False):
        dr, dc = SIDES[d]
        row = 0 if dr < 0 else R - 1
        land_row = R + 1 if dr < 0 else 0
        col = pl.ds(0, EDGE) if dc < 0 else pl.ds(W - EDGE, EDGE)
        side = 1 if dc < 0 else 0
        fr = 2 * which
        if dc == 0:
            rs, cs = pl.ds(row, 1), pl.ds(0, W)
            dst = F.at[cv, fr, pl.ds(land_row, 1), pl.ds(0, W)]
        elif dr == 0:
            rs, cs = pl.ds(0, R), col
            dst = L.at[cv, which, side, pl.ds(1, R)]
        else:
            rs, cs = pl.ds(row, 1), col
            dst = L.at[cv, which, side, pl.ds(land_row, 1)]
        if from_hbm:
            src = caches[cv].at[0, rs, cs]
        else:
            src = F.at[cv, fr, pl.ds(1 + rs.start, rs.size), cs]
        return pltpu.make_async_remote_copy(
            src_ref=src, dst_ref=dst, send_sem=send_sem.at[cv, which, d],
            recv_sem=recv_sem.at[cv, which, d], device_id=where_is(d), device_id_type=MESH)

    def send_sides(cv, which, ds, from_hbm=False):
        for d in ds:
            @pl.when(exists(d))
            def _():
                side_copy(cv, which, d, from_hbm).start()

    def recv_sides(cv, which, ds):
        for d in ds:
            opposite = SIDES.index((-SIDES[d][0], -SIDES[d][1]))

            @pl.when(exists(opposite))
            def _():
                side_copy(cv, which, d, which == 0).wait_recv()

    def drain_sides(cv, which):
        for d in range(8):
            @pl.when(exists(d))
            def _():
                side_copy(cv, which, d, which == 0).wait_send()

    partner = {"frm": 1 - f}

    def main_copy(cv, i, cache):
        here = pl.ds(1 + i * STEP, STEP)
        if cache:
            src = caches[cv].at[0, pl.ds(i * STEP, STEP)]
        else:
            src = F.at[cv, 2, here, pl.ds(0, W)]
        return pltpu.make_async_remote_copy(
            src_ref=src, dst_ref=F.at[cv, 1, here, pl.ds(0, W)], send_sem=mid_send.at[cv, i],
            recv_sem=mid_recv.at[cv, i], device_id=partner, device_id_type=MESH)

    payload = 2 * (1 - f)

    def rim_copy(cv, part):
        if part < 2:
            rs, cs = pl.ds((R + 1) * part, 1), pl.ds(0, WP)
        else:
            rs, cs = pl.ds(1, R), pl.ds(W, EDGE)
        return pltpu.make_async_remote_copy(
            src_ref=F.at[cv, payload, rs, cs], dst_ref=F.at[cv, 1, rs, cs],
            send_sem=mid_send.at[cv, blocks + part], recv_sem=mid_recv.at[cv, blocks + part],
            device_id=partner, device_id_type=MESH)

    def merge(cv, which, rs):
        left, right = L[cv, which, 0, rs], L[cv, which, 1, rs]
        place = lax.broadcasted_iota(jnp.int32, left.shape, 1)
        tile = jnp.where(place < EDGE // 2, right.astype(jnp.float32), left.astype(jnp.float32))
        F[cv, 2 * which, rs, pl.ds(W, EDGE)] = tile.astype(jnp.bfloat16)

    send_sides(0, 0, range(8), True)

    @pl.when(f == 1)
    def _():
        for i in range(blocks):
            main_copy(0, i, True).start()

    for cv in range(2):
        for which in range(2):
            for ok, row in ((up_ok, 0), (down_ok, R + 1)):
                @pl.when(jnp.logical_not(ok))
                def _():
                    F[cv, 2 * which, row, pl.ds(0, W)] = jnp.zeros((W, CH), jnp.bfloat16)

                for side, across in ((0, left_ok), (1, right_ok)):
                    @pl.when(jnp.logical_not(jnp.logical_and(ok, across)))
                    def _():
                        L[cv, which, side, row] = jnp.zeros((EDGE, CH), jnp.bfloat16)
            for side, across in ((0, left_ok), (1, right_ok)):
                @pl.when(jnp.logical_not(across))
                def _():
                    L[cv, which, side, pl.ds(1, R)] = jnp.zeros((R, EDGE, CH), jnp.bfloat16)

    lat_cp.wait()
    pw_cp.wait()

    def project(i, carry):
        v = jnp.dot(lat[i], pw[...], preferred_element_type=jnp.float32) + pb[...]
        v = v.astype(jnp.bfloat16).astype(jnp.float32)
        a = v / (1.0 + jnp.exp(-v))
        for k in range(2):
            s1[pl.ds(k, HW, stride=2), :] = v
            s2[pl.ds(k, HW, stride=2), :] = a
        up[i] = s1[...].astype(jnp.bfloat16)
        wide = s2[...].astype(jnp.bfloat16)
        F[0, 2, 1 + 2 * i, pl.ds(0, W)] = wide
        F[0, 2, 2 + 2 * i, pl.ds(0, W)] = wide
        return carry

    lax.fori_loop(0, HR, project, 0)
    send_sides(0, 1, range(8))

    @pl.when(f == 0)
    def _():
        for i in range(blocks):
            main_copy(0, i, False).start()

    send_sides(1, 0, range(8), True)

    @pl.when(f == 1)
    def _():
        for i in range(blocks):
            main_copy(1, i, True).start()

    def taps(cv, frames, base):
        lhs = jnp.concatenate(
            [F[cv, a, pl.ds(base + p, STEP)].reshape(STEP * WP, CH)
             for a in frames for p in range(3)], axis=1)
        rhs = jnp.concatenate([w[cv, a].reshape(3 * CH, 3 * CH) for a in frames], axis=0)
        return jnp.dot(lhs, rhs, preferred_element_type=jnp.float32)

    def fold(z, n):
        z = z[n * WP:(n + 1) * WP]
        return (pltpu.roll(z[:, :CH], 1, 0)[:W] + z[:W, CH:2 * CH]
                + pltpu.roll(z[:, 2 * CH:], WP - 1, 0)[:W])

    def begin(cv, frames, i):
        z = taps(cv, frames, i * STEP)
        for n in range(STEP):
            acc[i * STEP + n] = fold(z, n)

    def finish_one(i):
        base = i * STEP
        z = taps(0, (1,), base)
        for n in range(STEP):
            y = fold(z, n) + acc[base + n] + b1[...]
            F[1, 2, base + n + 1, pl.ds(0, W)] = (y / (1.0 + jnp.exp(-y))).astype(jnp.bfloat16)

        @pl.when(f == 0)
        def _():
            main_copy(1, i, False).start()

    def out_copy(i):
        here = pl.ds(i * STEP, STEP)
        return pltpu.make_async_copy(obuf.at[here], out_h.at[0, here], out_sem.at[i])

    def finish_two(i):
        base = i * STEP
        z = taps(1, (1, 2), base)
        for n in range(STEP):
            y = fold(z, n) + acc[base + n] + b2[...] + up[(base + n) // 2].astype(jnp.float32)
            obuf[base + n] = y.astype(jnp.bfloat16)
        out_copy(i).start()

    def each(body, start, count):
        def step(k, carry):
            body(lax.rem(start + k, blocks))
            return carry

        lax.fori_loop(0, count, step, 0)

    def inner(body):
        each(body, 1, blocks - 2)

    def outer(body):
        each(body, blocks - 1, 2)

    cols, tall_ds = (2, 3), (0, 1, 4, 5, 6, 7)
    body_rows, rims = pl.ds(1, R), (pl.ds(0, 1), pl.ds(R + 1, 1))

    cache_cp[0].wait()
    for cp in w_cp[0]:
        cp.wait()
    for which in range(2):
        recv_sides(0, which, cols)
        merge(0, which, body_rows)
    rim_copy(0, 2).start()
    inner(lambda i: begin(0, (0, 2), i))
    for which in range(2):
        recv_sides(0, which, tall_ds)
        for rs in rims:
            merge(0, which, rs)
    for part in range(2):
        rim_copy(0, part).start()
    outer(lambda i: begin(0, (0, 2), i))
    for i in range(blocks):
        main_copy(0, i, False).wait_recv()
    for part in range(3):
        rim_copy(0, part).wait_recv()
    outer(finish_one)
    send_sides(1, 1, tall_ds)
    inner(finish_one)
    send_sides(1, 1, cols)

    cache_cp[1].wait()
    for cp in w_cp[1]:
        cp.wait()
    recv_sides(1, 0, range(8))
    merge(1, 0, pl.ds(0, R + 2))

    @pl.when(f == 1)
    def _():
        for part in range(3):
            rim_copy(1, part).start()

    each(lambda i: begin(1, (0,), i), 0, blocks)
    recv_sides(1, 1, cols)
    merge(1, 1, body_rows)

    @pl.when(f == 0)
    def _():
        rim_copy(1, 2).start()

    for i in range(blocks):
        main_copy(1, i, False).wait_recv()
    rim_copy(1, 2).wait_recv()
    inner(finish_two)
    recv_sides(1, 1, tall_ds)
    for rs in rims:
        merge(1, 1, rs)

    @pl.when(f == 0)
    def _():
        for part in range(2):
            rim_copy(1, part).start()

    for part in range(2):
        rim_copy(1, part).wait_recv()
    outer(finish_two)

    for cv in range(2):
        for which in range(2):
            drain_sides(cv, which)
        for i in range(blocks):
            main_copy(cv, i, False).wait_send()
        for part in range(3):
            rim_copy(cv, part).wait_send()
    for i in range(blocks):
        out_copy(i).wait()


def per_device(latent, proj_weight, proj_bias, cache_one, cache_two,
               conv_one, bias_one, conv_two, bias_two):
    _, R, W, CH = cache_one.shape
    _, HR, HW, LCH = latent.shape
    blocks = R // STEP
    WP = W + EDGE
    anywhere = pl.BlockSpec(memory_space=pl.ANY)
    vmem = pl.BlockSpec(memory_space=pltpu.VMEM)
    bf = jnp.bfloat16
    return pl.pallas_call(
        functools.partial(kernel, lax.axis_size("row"), lax.axis_size("col")),
        out_shape=jax.ShapeDtypeStruct(cache_one.shape, bf),
        in_specs=[anywhere, anywhere, vmem, anywhere, anywhere, anywhere, vmem, anywhere, vmem],
        out_specs=anywhere,
        scratch_shapes=[
            pltpu.VMEM((HR, HW, LCH), bf),
            pltpu.VMEM((LCH, CH), bf),
            pltpu.VMEM((2, 3, 3, CH, 3 * CH), bf),
            pltpu.VMEM((2, 3, R + 2, WP, CH), bf),
            pltpu.VMEM((2, 2, 2, R + 2, EDGE, CH), bf),
            pltpu.VMEM((HR, W, CH), bf),
            pltpu.VMEM((R, W, CH), bf),
            pltpu.VMEM((R, W, CH), jnp.float32),
            pltpu.VMEM((W, CH), jnp.float32),
            pltpu.VMEM((W, CH), jnp.float32),
            pltpu.SemaphoreType.DMA((10,)),
            pltpu.SemaphoreType.DMA((2, 2, 8)),
            pltpu.SemaphoreType.DMA((2, 2, 8)),
            pltpu.SemaphoreType.DMA((2, blocks + 3)),
            pltpu.SemaphoreType.DMA((2, blocks + 3)),
            pltpu.SemaphoreType.DMA((blocks,)),
        ],
        compiler_params=pltpu.CompilerParams(
            collective_id=0, has_side_effects=True, vmem_limit_bytes=60 * 1024 * 1024),
        name="decoder_window",
    )(latent, proj_weight, proj_bias.reshape(1, CH), cache_one, cache_two,
      conv_one, bias_one.reshape(1, CH), conv_two, bias_two.reshape(1, CH))


def solution(mesh):
    placed = P(("grp", "frm"), "row", "col", None)
    return jax.shard_map(
        per_device,
        mesh=mesh,
        in_specs=(placed, P(), P(), placed, placed, P(), P(), P(), P()),
        out_specs=placed,
        check_vma=False,
    )
```

```python
import functools

import jax
import jax.numpy as jnp
from jax import lax
from jax.experimental import pallas as pl
from jax.experimental.pallas import tpu as pltpu
from jax.sharding import PartitionSpec as P

EDGE = 16
STEP = 2
MESH = pl.DeviceIdType.MESH
SIDES = [(-1, 0), (1, 0), (0, -1), (0, 1), (-1, -1), (-1, 1), (1, -1), (1, 1)]


def kernel(rows_n, cols_n, lat_h, pw_h, pb, c1_h, c2_h, w1_h, b1, w2_h, b2, out_h,
           lat, pw, w, F, S, L, up, obuf, acc, s1, s2,
           load_sem, send_sem, recv_sem, mid_send, mid_recv, out_sem):
    R, W = c1_h.shape[1], c1_h.shape[2]
    CH = c1_h.shape[3]
    HR, HW = lat.shape[0], lat.shape[1]
    blocks = R // STEP
    r, c, f = lax.axis_index("row"), lax.axis_index("col"), lax.axis_index("frm")
    caches = (c1_h, c2_h)
    up_ok, down_ok = r > 0, r < rows_n - 1
    left_ok, right_ok = c > 0, c < cols_n - 1

    def exists(d):
        dr, dc = SIDES[d]
        ok = None
        for test in ([up_ok] if dr < 0 else [down_ok] if dr > 0 else []) + (
                [left_ok] if dc < 0 else [right_ok] if dc > 0 else []):
            ok = test if ok is None else jnp.logical_and(ok, test)
        return ok

    def where_is(d):
        dr, dc = SIDES[d]
        ids = {}
        if dr:
            ids["row"] = r + dr
        if dc:
            ids["col"] = c + dc
        return ids

    loads = []

    def load(src, dst):
        cp = pltpu.make_async_copy(src, dst, load_sem.at[len(loads)])
        cp.start()
        loads.append(cp)
        return cp

    lat_cp = load(lat_h.at[0], lat)
    pw_cp = load(pw_h, pw)
    cache_cp = [load(caches[0].at[0], F.at[0, 0, pl.ds(1, R), pl.ds(0, W)])]
    w_cp = [[load(w1_h.at[:, :, q], w.at[0, :, :, :, pl.ds(q * CH, CH)]) for q in range(3)]]
    cache_cp.append(load(caches[1].at[0], F.at[1, 0, pl.ds(1, R), pl.ds(0, W)]))
    w_cp.append([load(w2_h.at[:, :, q], w.at[1, :, :, :, pl.ds(q * CH, CH)]) for q in range(3)])

    barrier = pltpu.get_barrier_semaphore()
    for d in range(8):
        @pl.when(exists(d))
        def _():
            pl.semaphore_signal(barrier, inc=1, device_id=where_is(d), device_id_type=MESH)
    pl.semaphore_signal(barrier, inc=1, device_id={"frm": 1 - f}, device_id_type=MESH)
    tall = 1 + up_ok.astype(jnp.int32) + down_ok.astype(jnp.int32)
    wide = 1 + left_ok.astype(jnp.int32) + right_ok.astype(jnp.int32)
    pl.semaphore_wait(barrier, tall * wide)

    def side_copy(cv, which, d, from_hbm=False):
        dr, dc = SIDES[d]
        row = 0 if dr < 0 else R - 1
        land_row = R + 1 if dr < 0 else 0
        col = pl.ds(0, EDGE) if dc < 0 else pl.ds(W - EDGE, EDGE)
        side = 1 if dc < 0 else 0
        fr = 2 * which
        if dc == 0:
            rs, cs = pl.ds(row, 1), pl.ds(0, W)
            dst = F.at[cv, fr, pl.ds(land_row, 1), pl.ds(0, W)]
        elif dr == 0:
            rs, cs = pl.ds(0, R), col
            dst = L.at[cv, which, side, pl.ds(1, R)]
        else:
            rs, cs = pl.ds(row, 1), col
            dst = L.at[cv, which, side, pl.ds(land_row, 1)]
        if from_hbm:
            src = caches[cv].at[0, rs, cs]
        else:
            src = F.at[cv, fr, pl.ds(1 + rs.start, rs.size), cs]
        return pltpu.make_async_remote_copy(
            src_ref=src, dst_ref=dst, send_sem=send_sem.at[cv, which, d],
            recv_sem=recv_sem.at[cv, which, d], device_id=where_is(d), device_id_type=MESH)

    def send_sides(cv, which, ds, from_hbm=False):
        for d in ds:
            @pl.when(exists(d))
            def _():
                side_copy(cv, which, d, from_hbm).start()

    def recv_sides(cv, which, ds):
        for d in ds:
            opposite = SIDES.index((-SIDES[d][0], -SIDES[d][1]))

            @pl.when(exists(opposite))
            def _():
                side_copy(cv, which, d, which == 0).wait_recv()

    def drain_sides(cv, which):
        for d in range(8):
            @pl.when(exists(d))
            def _():
                side_copy(cv, which, d, which == 0).wait_send()

    partner = {"frm": 1 - f}

    def main_copy(cv, i, cache):
        here = pl.ds(1 + i * STEP, STEP)
        if cache:
            src = caches[cv].at[0, pl.ds(i * STEP, STEP)]
        else:
            src = F.at[cv, 2, here, pl.ds(0, W)]
        return pltpu.make_async_remote_copy(
            src_ref=src, dst_ref=F.at[cv, 1, here, pl.ds(0, W)], send_sem=mid_send.at[cv, i],
            recv_sem=mid_recv.at[cv, i], device_id=partner, device_id_type=MESH)

    payload = 2 * (1 - f)

    def rim_copy(cv, part):
        if part < 2:
            src, dst = (F.at[cv, fr, pl.ds((R + 1) * part, 1)] for fr in (payload, 1))
        else:
            src, dst = (S.at[cv, fr] for fr in (payload, 1))
        return pltpu.make_async_remote_copy(
            src_ref=src, dst_ref=dst,
            send_sem=mid_send.at[cv, blocks + part], recv_sem=mid_recv.at[cv, blocks + part],
            device_id=partner, device_id_type=MESH)

    def merge(cv, which):
        left, right = L[cv, which, 0], L[cv, which, 1]
        place = lax.broadcasted_iota(jnp.int32, left.shape, 1)
        tile = jnp.where(place < EDGE // 2, right.astype(jnp.float32), left.astype(jnp.float32))
        S[cv, 2 * which] = tile.astype(jnp.bfloat16)

    send_sides(0, 0, range(8), True)

    @pl.when(f == 1)
    def _():
        for i in range(blocks):
            main_copy(0, i, True).start()

    for cv in range(2):
        for which in range(2):
            for ok, row in ((up_ok, 0), (down_ok, R + 1)):
                @pl.when(jnp.logical_not(ok))
                def _():
                    F[cv, 2 * which, row, pl.ds(0, W)] = jnp.zeros((W, CH), jnp.bfloat16)

                for side, across in ((0, left_ok), (1, right_ok)):
                    @pl.when(jnp.logical_not(jnp.logical_and(ok, across)))
                    def _():
                        L[cv, which, side, row] = jnp.zeros((EDGE, CH), jnp.bfloat16)
            for side, across in ((0, left_ok), (1, right_ok)):
                @pl.when(jnp.logical_not(across))
                def _():
                    L[cv, which, side, pl.ds(1, R)] = jnp.zeros((R, EDGE, CH), jnp.bfloat16)

    lat_cp.wait()
    pw_cp.wait()

    def project(i, carry):
        v = jnp.dot(lat[i], pw[...], preferred_element_type=jnp.float32) + pb[...]
        v = v.astype(jnp.bfloat16).astype(jnp.float32)
        a = v / (1.0 + jnp.exp(-v))
        for k in range(2):
            s1[pl.ds(k, HW, stride=2), :] = v
            s2[pl.ds(k, HW, stride=2), :] = a
        up[i] = s1[...].astype(jnp.bfloat16)
        wide = s2[...].astype(jnp.bfloat16)
        F[0, 2, 1 + 2 * i, pl.ds(0, W)] = wide
        F[0, 2, 2 + 2 * i, pl.ds(0, W)] = wide
        return carry

    lax.fori_loop(0, HR, project, 0)
    send_sides(0, 1, range(8))

    @pl.when(f == 0)
    def _():
        for i in range(blocks):
            main_copy(0, i, False).start()

    send_sides(1, 0, range(8), True)

    @pl.when(f == 1)
    def _():
        for i in range(blocks):
            main_copy(1, i, True).start()

    def weights(cv, frames):
        return jnp.concatenate([w[cv, a].reshape(3 * CH, 3 * CH) for a in frames], axis=0)

    def taps(cv, frames, i):
        lhs = jnp.concatenate(
            [F[cv, a, pl.ds(i * STEP + p, STEP)].reshape(STEP * W, CH)
             for a in frames for p in range(3)], axis=1)
        return jnp.dot(lhs, weights(cv, frames), preferred_element_type=jnp.float32)

    spot = lax.broadcasted_iota(jnp.int32, (8, CH), 0)

    def fold(z, n):
        z = z[n * W:(n + 1) * W]
        after = pltpu.roll(z[:, :CH], 1, 0)
        after = jnp.concatenate([jnp.where(spot == 0, 0.0, after[:8]), after[8:]], axis=0)
        ahead = pltpu.roll(z[:, 2 * CH:], W - 1, 0)
        ahead = jnp.concatenate([ahead[:W - 8], jnp.where(spot == 7, 0.0, ahead[W - 8:])], axis=0)
        return after + z[:, CH:2 * CH] + ahead

    def begin(cv, frames):
        def body(i):
            z = taps(cv, frames, i)
            for n in range(STEP):
                acc[i * STEP + n] = fold(z, n)
        return body

    def more(cv, frames):
        def body(i):
            z = taps(cv, frames, i)
            for n in range(STEP):
                acc[i * STEP + n] += fold(z, n)
        return body

    def sides(cv):
        lhs = jnp.concatenate(
            [S[cv, a, pl.ds(p, R)].reshape(R * EDGE, CH) for a in range(3) for p in range(3)],
            axis=1)
        z = jnp.dot(lhs, weights(cv, range(3)), preferred_element_type=jnp.float32)
        for n in range(R):
            part = z[n * EDGE:(n + 1) * EDGE]
            acc[n, pl.ds(0, 1)] += part[EDGE - 1:, :CH]
            acc[n, pl.ds(W - 1, 1)] += part[:1, 2 * CH:]

    def finish_one(i):
        for n in range(STEP):
            y = acc[i * STEP + n] + b1[...]
            F[1, 2, i * STEP + n + 1] = (y / (1.0 + jnp.exp(-y))).astype(jnp.bfloat16)

        @pl.when(f == 0)
        def _():
            main_copy(1, i, False).start()

    def out_copy(i):
        here = pl.ds(i * STEP, STEP)
        return pltpu.make_async_copy(obuf.at[here], out_h.at[0, here], out_sem.at[i])

    def finish_two(i):
        base = i * STEP
        for n in range(STEP):
            y = acc[base + n] + b2[...] + up[(base + n) // 2].astype(jnp.float32)
            obuf[base + n] = y.astype(jnp.bfloat16)
        out_copy(i).start()

    def each(body, start, count):
        def step(k, carry):
            body(lax.rem(start + k, blocks))
            return carry

        lax.fori_loop(0, count, step, 0)

    def inner(body):
        each(body, 1, blocks - 2)

    def outer(body):
        each(body, blocks - 1, 2)

    cols, tall_ds = (2, 3), (0, 1, 4, 5, 6, 7)

    def mids(cv):
        for i in range(blocks):
            main_copy(cv, i, False).wait_recv()

    cache_cp[0].wait()
    for cp in w_cp[0]:
        cp.wait()
    inner(begin(0, (0, 2)))
    mids(0)
    inner(more(0, (1,)))
    for which in range(2):
        recv_sides(0, which, range(8))
        merge(0, which)
    for part in range(3):
        rim_copy(0, part).start()
    outer(begin(0, (0, 2)))
    for part in range(3):
        rim_copy(0, part).wait_recv()
    outer(more(0, (1,)))
    sides(0)
    outer(finish_one)
    send_sides(1, 1, tall_ds)
    inner(finish_one)
    send_sides(1, 1, cols)

    cache_cp[1].wait()
    for cp in w_cp[1]:
        cp.wait()
    recv_sides(1, 0, range(8))
    merge(1, 0)

    @pl.when(f == 1)
    def _():
        for part in range(3):
            rim_copy(1, part).start()

    each(begin(1, (0,)), 0, blocks)
    mids(1)
    inner(more(1, (1, 2)))
    recv_sides(1, 1, range(8))
    merge(1, 1)

    @pl.when(f == 0)
    def _():
        for part in range(3):
            rim_copy(1, part).start()

    outer(more(1, (2,)))
    for part in range(3):
        rim_copy(1, part).wait_recv()
    sides(1)
    inner(finish_two)
    outer(more(1, (1,)))
    outer(finish_two)

    for cv in range(2):
        for which in range(2):
            drain_sides(cv, which)
        for i in range(blocks):
            main_copy(cv, i, False).wait_send()
        for part in range(3):
            rim_copy(cv, part).wait_send()
    for i in range(blocks):
        out_copy(i).wait()


def per_device(latent, proj_weight, proj_bias, cache_one, cache_two,
               conv_one, bias_one, conv_two, bias_two):
    _, R, W, CH = cache_one.shape
    _, HR, HW, LCH = latent.shape
    blocks = R // STEP
    anywhere = pl.BlockSpec(memory_space=pl.ANY)
    vmem = pl.BlockSpec(memory_space=pltpu.VMEM)
    bf = jnp.bfloat16
    return pl.pallas_call(
        functools.partial(kernel, lax.axis_size("row"), lax.axis_size("col")),
        out_shape=jax.ShapeDtypeStruct(cache_one.shape, bf),
        in_specs=[anywhere, anywhere, vmem, anywhere, anywhere, anywhere, vmem, anywhere, vmem],
        out_specs=anywhere,
        scratch_shapes=[
            pltpu.VMEM((HR, HW, LCH), bf),
            pltpu.VMEM((LCH, CH), bf),
            pltpu.VMEM((2, 3, 3, CH, 3 * CH), bf),
            pltpu.VMEM((2, 3, R + 2, W, CH), bf),
            pltpu.VMEM((2, 3, R + 2, EDGE, CH), bf),
            pltpu.VMEM((2, 2, 2, R + 2, EDGE, CH), bf),
            pltpu.VMEM((HR, W, CH), bf),
            pltpu.VMEM((R, W, CH), bf),
            pltpu.VMEM((R, W, CH), jnp.float32),
            pltpu.VMEM((W, CH), jnp.float32),
            pltpu.VMEM((W, CH), jnp.float32),
            pltpu.SemaphoreType.DMA((10,)),
            pltpu.SemaphoreType.DMA((2, 2, 8)),
            pltpu.SemaphoreType.DMA((2, 2, 8)),
            pltpu.SemaphoreType.DMA((2, blocks + 3)),
            pltpu.SemaphoreType.DMA((2, blocks + 3)),
            pltpu.SemaphoreType.DMA((blocks,)),
        ],
        compiler_params=pltpu.CompilerParams(
            collective_id=0, has_side_effects=True, vmem_limit_bytes=60 * 1024 * 1024),
        name="decoder_window",
    )(latent, proj_weight, proj_bias.reshape(1, CH), cache_one, cache_two,
      conv_one, bias_one.reshape(1, CH), conv_two, bias_two.reshape(1, CH))


def solution(mesh):
    placed = P(("grp", "frm"), "row", "col", None)
    return jax.shard_map(
        per_device,
        mesh=mesh,
        in_specs=(placed, P(), P(), placed, placed, P(), P(), P(), P()),
        out_specs=placed,
        check_vma=False,
    )
```

```python
import functools

import jax
import jax.numpy as jnp
from jax import lax
from jax.experimental import pallas as pl
from jax.experimental.pallas import tpu as pltpu
from jax.sharding import PartitionSpec as P

EDGE = 16
STEP = 1
MESH = pl.DeviceIdType.MESH
SIDES = [(-1, 0), (1, 0), (0, -1), (0, 1), (-1, -1), (-1, 1), (1, -1), (1, 1)]


def kernel(rows_n, cols_n, lat_h, pw_h, pb, c1_h, c2_h, w1_h, b1, w2_h, b2, out_h,
           lat, pw, w, F, S, L, up, obuf, acc, ca, CL, s1, s2,
           load_sem, send_sem, recv_sem, mid_send, mid_recv, out_sem):
    R, W = c1_h.shape[1], c1_h.shape[2]
    CH = c1_h.shape[3]
    HR, HW = lat.shape[0], lat.shape[1]
    blocks = R // STEP
    r, c, f = lax.axis_index("row"), lax.axis_index("col"), lax.axis_index("frm")
    caches = (c1_h, c2_h)
    up_ok, down_ok = r > 0, r < rows_n - 1
    left_ok, right_ok = c > 0, c < cols_n - 1

    def exists(d):
        dr, dc = SIDES[d]
        ok = None
        for test in ([up_ok] if dr < 0 else [down_ok] if dr > 0 else []) + (
                [left_ok] if dc < 0 else [right_ok] if dc > 0 else []):
            ok = test if ok is None else jnp.logical_and(ok, test)
        return ok

    def where_is(d):
        dr, dc = SIDES[d]
        ids = {}
        if dr:
            ids["row"] = r + dr
        if dc:
            ids["col"] = c + dc
        return ids

    loads = []

    def load(src, dst):
        cp = pltpu.make_async_copy(src, dst, load_sem.at[len(loads)])
        cp.start()
        loads.append(cp)
        return cp

    lat_cp = load(lat_h.at[0], lat)
    pw_cp = load(pw_h, pw)
    cache_cp = [load(caches[0].at[0], F.at[0, 0, pl.ds(1, R), pl.ds(0, W)])]
    w_cp = [[load(w1_h.at[:, :, q], w.at[0, :, :, :, pl.ds(q * CH, CH)]) for q in range(3)]]
    cache_cp.append(load(caches[1].at[0], F.at[1, 0, pl.ds(1, R), pl.ds(0, W)]))
    w_cp.append([load(w2_h.at[:, :, q], w.at[1, :, :, :, pl.ds(q * CH, CH)]) for q in range(3)])

    barrier = pltpu.get_barrier_semaphore()
    for d in range(8):
        @pl.when(exists(d))
        def _():
            pl.semaphore_signal(barrier, inc=1, device_id=where_is(d), device_id_type=MESH)
    pl.semaphore_signal(barrier, inc=1, device_id={"frm": 1 - f}, device_id_type=MESH)
    tall = 1 + up_ok.astype(jnp.int32) + down_ok.astype(jnp.int32)
    wide = 1 + left_ok.astype(jnp.int32) + right_ok.astype(jnp.int32)
    pl.semaphore_wait(barrier, tall * wide)

    def side_copy(cv, which, d, from_hbm=False):
        dr, dc = SIDES[d]
        row = 0 if dr < 0 else R - 1
        land_row = R + 1 if dr < 0 else 0
        col = pl.ds(0, EDGE) if dc < 0 else pl.ds(W - EDGE, EDGE)
        side = 1 if dc < 0 else 0
        fr = 2 * which
        if dc == 0:
            rs, cs = pl.ds(row, 1), pl.ds(0, W)
            dst = F.at[cv, fr, pl.ds(land_row, 1), pl.ds(0, W)]
        elif dr == 0:
            rs, cs = pl.ds(0, R), col
            dst = L.at[cv, which, side, pl.ds(1, R)]
        else:
            rs, cs = pl.ds(row, 1), col
            dst = L.at[cv, which, side, pl.ds(land_row, 1)]
        if cv == 0 and which == 1 and dc == 0:
            src = ca.at[pl.ds(0 if dr < 0 else HR - 1, 1)]
            dst = CL.at[pl.ds(1 if dr < 0 else 0, 1)]
        elif from_hbm:
            src = caches[cv].at[0, rs, cs]
        else:
            src = F.at[cv, fr, pl.ds(1 + rs.start, rs.size), cs]
        return pltpu.make_async_remote_copy(
            src_ref=src, dst_ref=dst, send_sem=send_sem.at[cv, which, d],
            recv_sem=recv_sem.at[cv, which, d], device_id=where_is(d), device_id_type=MESH)

    def send_sides(cv, which, ds, from_hbm=False):
        for d in ds:
            @pl.when(exists(d))
            def _():
                side_copy(cv, which, d, from_hbm).start()

    def recv_sides(cv, which, ds):
        for d in ds:
            opposite = SIDES.index((-SIDES[d][0], -SIDES[d][1]))

            @pl.when(exists(opposite))
            def _():
                side_copy(cv, which, d, which == 0).wait_recv()

    def drain_sides(cv, which):
        for d in range(8):
            @pl.when(exists(d))
            def _():
                side_copy(cv, which, d, which == 0).wait_send()

    partner = {"frm": 1 - f}

    def main_copy(cv, i, cache):
        here = pl.ds(1 + i * STEP, STEP)
        if cache:
            src = caches[cv].at[0, pl.ds(i * STEP, STEP)]
        else:
            src = F.at[cv, 2, here, pl.ds(0, W)]
        return pltpu.make_async_remote_copy(
            src_ref=src, dst_ref=F.at[cv, 1, here, pl.ds(0, W)], send_sem=mid_send.at[cv, i],
            recv_sem=mid_recv.at[cv, i], device_id=partner, device_id_type=MESH)

    payload = 2 * (1 - f)

    def rim_copy(cv, part):
        if part < 2:
            src, dst = (F.at[cv, fr, pl.ds((R + 1) * part, 1)] for fr in (payload, 1))
        else:
            src, dst = (S.at[cv, fr] for fr in (payload, 1))
        return pltpu.make_async_remote_copy(
            src_ref=src, dst_ref=dst,
            send_sem=mid_send.at[cv, blocks + part], recv_sem=mid_recv.at[cv, blocks + part],
            device_id=partner, device_id_type=MESH)

    def merge(cv, which):
        left, right = L[cv, which, 0], L[cv, which, 1]
        place = lax.broadcasted_iota(jnp.int32, left.shape, 1)
        tile = jnp.where(place < EDGE // 2, right.astype(jnp.float32), left.astype(jnp.float32))
        S[cv, 2 * which] = tile.astype(jnp.bfloat16)

    send_sides(0, 0, range(8), True)

    @pl.when(f == 1)
    def _():
        for i in range(blocks):
            main_copy(0, i, True).start()

    for cv in range(2):
        for which in range(2):
            for ok, row in ((up_ok, 0), (down_ok, R + 1)):
                @pl.when(jnp.logical_not(ok))
                def _():
                    F[cv, 2 * which, row, pl.ds(0, W)] = jnp.zeros((W, CH), jnp.bfloat16)

                for side, across in ((0, left_ok), (1, right_ok)):
                    @pl.when(jnp.logical_not(jnp.logical_and(ok, across)))
                    def _():
                        L[cv, which, side, row] = jnp.zeros((EDGE, CH), jnp.bfloat16)
            for side, across in ((0, left_ok), (1, right_ok)):
                @pl.when(jnp.logical_not(across))
                def _():
                    L[cv, which, side, pl.ds(1, R)] = jnp.zeros((R, EDGE, CH), jnp.bfloat16)

    lat_cp.wait()
    pw_cp.wait()

    def project(i, carry):
        v = jnp.dot(lat[i], pw[...], preferred_element_type=jnp.float32) + pb[...]
        v = v.astype(jnp.bfloat16).astype(jnp.float32)
        a = v / (1.0 + jnp.exp(-v))
        ca[i] = a.astype(jnp.bfloat16)
        for k in range(2):
            s1[pl.ds(k, HW, stride=2), :] = v
            s2[pl.ds(k, HW, stride=2), :] = a
        up[i] = s1[...].astype(jnp.bfloat16)
        wide = s2[...].astype(jnp.bfloat16)
        F[0, 2, 1 + 2 * i, pl.ds(0, W)] = wide
        F[0, 2, 2 + 2 * i, pl.ds(0, W)] = wide
        return carry

    lax.fori_loop(0, HR, project, 0)
    send_sides(0, 1, range(8))

    @pl.when(f == 0)
    def _():
        for i in range(blocks):
            main_copy(0, i, False).start()

    send_sides(1, 0, range(8), True)

    @pl.when(f == 1)
    def _():
        for i in range(blocks):
            main_copy(1, i, True).start()

    def weights(cv, frames):
        return jnp.concatenate([w[cv, a].reshape(3 * CH, 3 * CH) for a in frames], axis=0)

    def taps(cv, frames, i):
        lhs = jnp.concatenate(
            [F[cv, a, pl.ds(i * STEP + p, STEP)].reshape(STEP * W, CH)
             for a in frames for p in range(3)], axis=1)
        return jnp.dot(lhs, weights(cv, frames), preferred_element_type=jnp.float32)

    spot = lax.broadcasted_iota(jnp.int32, (8, CH), 0)

    def fold(z, n):
        z = z[n * W:(n + 1) * W]
        after = pltpu.roll(z[:, :CH], 1, 0)
        after = jnp.concatenate([jnp.where(spot == 0, 0.0, after[:8]), after[8:]], axis=0)
        ahead = pltpu.roll(z[:, 2 * CH:], W - 1, 0)
        ahead = jnp.concatenate([ahead[:W - 8], jnp.where(spot == 7, 0.0, ahead[W - 8:])], axis=0)
        return after + z[:, CH:2 * CH] + ahead

    def begin(cv, frames):
        def body(i):
            z = taps(cv, frames, i)
            for n in range(STEP):
                acc[i * STEP + n] = fold(z, n)
        return body

    def more(cv, frames):
        def body(i):
            z = taps(cv, frames, i)
            for n in range(STEP):
                acc[i * STEP + n] += fold(z, n)
        return body

    def sides(cv):
        lhs = jnp.concatenate(
            [S[cv, a, pl.ds(p, R)].reshape(R * EDGE, CH) for a in range(3) for p in range(3)],
            axis=1)
        z = jnp.dot(lhs, weights(cv, range(3)), preferred_element_type=jnp.float32)
        for n in range(R):
            part = z[n * EDGE:(n + 1) * EDGE]
            acc[n, pl.ds(0, 1)] += part[EDGE - 1:, :CH]
            acc[n, pl.ds(W - 1, 1)] += part[:1, 2 * CH:]

    def finish_one(i):
        for n in range(STEP):
            y = acc[i * STEP + n] + b1[...]
            F[1, 2, i * STEP + n + 1] = (y / (1.0 + jnp.exp(-y))).astype(jnp.bfloat16)

        @pl.when(f == 0)
        def _():
            main_copy(1, i, False).start()

    def out_copy(i):
        here = pl.ds(i * STEP, STEP)
        return pltpu.make_async_copy(obuf.at[here], out_h.at[0, here], out_sem.at[i])

    def finish_two(i):
        base = i * STEP
        for n in range(STEP):
            y = acc[base + n] + b2[...] + up[(base + n) // 2].astype(jnp.float32)
            obuf[base + n] = y.astype(jnp.bfloat16)
        out_copy(i).start()

    def each(body, start, count):
        def step(k, carry):
            body(lax.rem(start + k, blocks))
            return carry

        lax.fori_loop(0, count, step, 0)

    def inner(body):
        each(body, 1, blocks - 2)

    def outer(body):
        each(body, blocks - 1, 2)

    cols, tall_ds = (2, 3), (0, 1, 4, 5, 6, 7)

    def mids(cv):
        for i in range(blocks):
            main_copy(cv, i, False).wait_recv()

    cache_cp[0].wait()
    for cp in w_cp[0]:
        cp.wait()
    inner(begin(0, (0, 2)))
    mids(0)
    inner(more(0, (1,)))
    recv_sides(0, 0, range(8))
    merge(0, 0)

    @pl.when(f == 1)
    def _():
        for part in range(3):
            rim_copy(0, part).start()

    recv_sides(0, 1, range(8))
    merge(0, 1)
    for k, ok in ((0, up_ok), (1, down_ok)):
        @pl.when(ok)
        def _():
            a = CL[k].astype(jnp.float32)
            for n in range(2):
                s2[pl.ds(n, HW, stride=2), :] = a
            F[0, 2, k * (R + 1)] = s2[...].astype(jnp.bfloat16)

    @pl.when(f == 0)
    def _():
        for part in range(3):
            rim_copy(0, part).start()

    outer(begin(0, (0, 2)))
    for part in range(3):
        rim_copy(0, part).wait_recv()
    outer(more(0, (1,)))
    sides(0)
    outer(finish_one)
    send_sides(1, 1, tall_ds)
    inner(finish_one)
    send_sides(1, 1, cols)

    cache_cp[1].wait()
    for cp in w_cp[1]:
        cp.wait()
    recv_sides(1, 0, range(8))
    merge(1, 0)

    @pl.when(f == 1)
    def _():
        for part in range(3):
            rim_copy(1, part).start()

    each(begin(1, (0,)), 0, blocks)
    mids(1)
    inner(more(1, (1, 2)))
    recv_sides(1, 1, range(8))
    merge(1, 1)

    @pl.when(f == 0)
    def _():
        for part in range(3):
            rim_copy(1, part).start()

    outer(more(1, (2,)))
    for part in range(3):
        rim_copy(1, part).wait_recv()
    sides(1)
    inner(finish_two)
    outer(more(1, (1,)))
    outer(finish_two)

    for cv in range(2):
        for which in range(2):
            drain_sides(cv, which)
        for i in range(blocks):
            main_copy(cv, i, False).wait_send()
        for part in range(3):
            rim_copy(cv, part).wait_send()
    for i in range(blocks):
        out_copy(i).wait()


def per_device(latent, proj_weight, proj_bias, cache_one, cache_two,
               conv_one, bias_one, conv_two, bias_two):
    _, R, W, CH = cache_one.shape
    _, HR, HW, LCH = latent.shape
    blocks = R // STEP
    anywhere = pl.BlockSpec(memory_space=pl.ANY)
    vmem = pl.BlockSpec(memory_space=pltpu.VMEM)
    bf = jnp.bfloat16
    return pl.pallas_call(
        functools.partial(kernel, lax.axis_size("row"), lax.axis_size("col")),
        out_shape=jax.ShapeDtypeStruct(cache_one.shape, bf),
        in_specs=[anywhere, anywhere, vmem, anywhere, anywhere, anywhere, vmem, anywhere, vmem],
        out_specs=anywhere,
        scratch_shapes=[
            pltpu.VMEM((HR, HW, LCH), bf),
            pltpu.VMEM((LCH, CH), bf),
            pltpu.VMEM((2, 3, 3, CH, 3 * CH), bf),
            pltpu.VMEM((2, 3, R + 2, W, CH), bf),
            pltpu.VMEM((2, 3, R + 2, EDGE, CH), bf),
            pltpu.VMEM((2, 2, 2, R + 2, EDGE, CH), bf),
            pltpu.VMEM((HR, W, CH), bf),
            pltpu.VMEM((R, W, CH), bf),
            pltpu.VMEM((R, W, CH), jnp.float32),
            pltpu.VMEM((HR, HW, CH), bf),
            pltpu.VMEM((2, HW, CH), bf),
            pltpu.VMEM((W, CH), jnp.float32),
            pltpu.VMEM((W, CH), jnp.float32),
            pltpu.SemaphoreType.DMA((10,)),
            pltpu.SemaphoreType.DMA((2, 2, 8)),
            pltpu.SemaphoreType.DMA((2, 2, 8)),
            pltpu.SemaphoreType.DMA((2, blocks + 3)),
            pltpu.SemaphoreType.DMA((2, blocks + 3)),
            pltpu.SemaphoreType.DMA((blocks,)),
        ],
        compiler_params=pltpu.CompilerParams(
            collective_id=0, has_side_effects=True, vmem_limit_bytes=60 * 1024 * 1024),
        name="decoder_window",
    )(latent, proj_weight, proj_bias.reshape(1, CH), cache_one, cache_two,
      conv_one, bias_one.reshape(1, CH), conv_two, bias_two.reshape(1, CH))


def solution(mesh):
    placed = P(("grp", "frm"), "row", "col", None)
    return jax.shard_map(
        per_device,
        mesh=mesh,
        in_specs=(placed, P(), P(), placed, placed, P(), P(), P(), P()),
        out_specs=placed,
        check_vma=False,
    )
```

```python
import functools

import jax
import jax.numpy as jnp
from jax import lax
from jax.experimental import pallas as pl
from jax.experimental.pallas import tpu as pltpu
from jax.sharding import PartitionSpec as P

EDGE = 16
STEP = 1
GROUP = 2
MESH = pl.DeviceIdType.MESH
SIDES = [(-1, 0), (1, 0), (0, -1), (0, 1), (-1, -1), (-1, 1), (1, -1), (1, 1)]


def kernel(rows_n, cols_n, lat_h, pw_h, pb_h, c1_h, c2_h, w1_h, b1_h, w2_h, b2_h, out_h,

           lat, pw, w, F, S, L, up, obuf, acc, ca, CL, s1, s2, pb, b1, b2,
           load_sem, send_sem, recv_sem, mid_send, mid_recv, out_sem):
    R, W = c1_h.shape[1], c1_h.shape[2]
    CH = c1_h.shape[3]
    HR, HW = lat.shape[0], lat.shape[1]
    blocks = R // STEP
    r, c, f = lax.axis_index("row"), lax.axis_index("col"), lax.axis_index("frm")
    caches = (c1_h, c2_h)
    up_ok, down_ok = r > 0, r < rows_n - 1
    left_ok, right_ok = c > 0, c < cols_n - 1

    def exists(d):
        dr, dc = SIDES[d]
        ok = None
        for test in ([up_ok] if dr < 0 else [down_ok] if dr > 0 else []) + (
                [left_ok] if dc < 0 else [right_ok] if dc > 0 else []):
            ok = test if ok is None else jnp.logical_and(ok, test)
        return ok

    def where_is(d):
        dr, dc = SIDES[d]
        ids = {}
        if dr:
            ids["row"] = r + dr
        if dc:
            ids["col"] = c + dc
        return ids

    loads = []

    def load(src, dst):
        cp = pltpu.make_async_copy(src, dst, load_sem.at[len(loads)])
        cp.start()
        loads.append(cp)
        return cp

    lat_cp = load(lat_h.at[0], lat)
    pw_cp = load(pw_h, pw)
    bias_cp = [load(src, dst) for src, dst in ((pb_h, pb), (b1_h, b1), (b2_h, b2))]
    cache_cp = [load(caches[0].at[0], F.at[0, 0, pl.ds(1, R), pl.ds(0, W)])]
    w_cp = [[load(w1_h.at[:, :, q], w.at[0, :, :, :, pl.ds(q * CH, CH)]) for q in range(3)]]
    cache_cp.append(load(caches[1].at[0], F.at[1, 0, pl.ds(1, R), pl.ds(0, W)]))
    w_cp.append([load(w2_h.at[:, :, q], w.at[1, :, :, :, pl.ds(q * CH, CH)]) for q in range(3)])

    barrier = pltpu.get_barrier_semaphore()
    for d in range(8):
        @pl.when(exists(d))
        def _():
            pl.semaphore_signal(barrier, inc=1, device_id=where_is(d), device_id_type=MESH)
    pl.semaphore_signal(barrier, inc=1, device_id={"frm": 1 - f}, device_id_type=MESH)
    tall = 1 + up_ok.astype(jnp.int32) + down_ok.astype(jnp.int32)
    wide = 1 + left_ok.astype(jnp.int32) + right_ok.astype(jnp.int32)
    pl.semaphore_wait(barrier, tall * wide)

    def side_copy(cv, which, d, from_hbm=False):
        dr, dc = SIDES[d]
        row = 0 if dr < 0 else R - 1
        land_row = R + 1 if dr < 0 else 0
        col = pl.ds(0, EDGE) if dc < 0 else pl.ds(W - EDGE, EDGE)
        side = 1 if dc < 0 else 0
        fr = 2 * which
        if dc == 0:
            rs, cs = pl.ds(row, 1), pl.ds(0, W)
            dst = F.at[cv, fr, pl.ds(land_row, 1), pl.ds(0, W)]
        elif dr == 0:
            rs, cs = pl.ds(0, R), col
            dst = L.at[cv, which, side, pl.ds(1, R)]
        else:
            rs, cs = pl.ds(row, 1), col
            dst = L.at[cv, which, side, pl.ds(land_row, 1)]
        if cv == 0 and which == 1 and dc == 0:
            src = ca.at[pl.ds(0 if dr < 0 else HR - 1, 1)]
            dst = CL.at[pl.ds(1 if dr < 0 else 0, 1)]
        elif from_hbm:
            src = caches[cv].at[0, rs, cs]
        else:
            src = F.at[cv, fr, pl.ds(1 + rs.start, rs.size), cs]
        return pltpu.make_async_remote_copy(
            src_ref=src, dst_ref=dst, send_sem=send_sem.at[cv, which, d],
            recv_sem=recv_sem.at[cv, which, d], device_id=where_is(d), device_id_type=MESH)

    def send_sides(cv, which, ds, from_hbm=False):
        for d in ds:
            @pl.when(exists(d))
            def _():
                side_copy(cv, which, d, from_hbm).start()

    def recv_sides(cv, which, ds):
        for d in ds:
            opposite = SIDES.index((-SIDES[d][0], -SIDES[d][1]))

            @pl.when(exists(opposite))
            def _():
                side_copy(cv, which, d, which == 0).wait_recv()

    def drain_sides(cv, which):
        for d in range(8):
            @pl.when(exists(d))
            def _():
                side_copy(cv, which, d, which == 0).wait_send()

    partner = {"frm": 1 - f}

    def main_copy(cv, i, cache):
        here = pl.ds(1 + i * STEP, STEP)
        if cache:
            src = caches[cv].at[0, pl.ds(i * STEP, STEP)]
        else:
            src = F.at[cv, 2, here, pl.ds(0, W)]
        return pltpu.make_async_remote_copy(
            src_ref=src, dst_ref=F.at[cv, 1, here, pl.ds(0, W)], send_sem=mid_send.at[cv, i],
            recv_sem=mid_recv.at[cv, i], device_id=partner, device_id_type=MESH)

    payload = 2 * (1 - f)

    def rim_copy(cv, part):
        if part < 2:
            src, dst = (F.at[cv, fr, pl.ds((R + 1) * part, 1)] for fr in (payload, 1))
        else:
            src, dst = (S.at[cv, fr] for fr in (payload, 1))
        return pltpu.make_async_remote_copy(
            src_ref=src, dst_ref=dst,
            send_sem=mid_send.at[cv, blocks + part], recv_sem=mid_recv.at[cv, blocks + part],
            device_id=partner, device_id_type=MESH)

    def merge(cv, which):
        left, right = L[cv, which, 0], L[cv, which, 1]
        place = lax.broadcasted_iota(jnp.int32, left.shape, 1)
        tile = jnp.where(place < EDGE // 2, right.astype(jnp.float32), left.astype(jnp.float32))
        S[cv, 2 * which] = tile.astype(jnp.bfloat16)

    send_sides(0, 0, range(8), True)

    @pl.when(f == 1)
    def _():
        for i in range(blocks):
            main_copy(0, i, True).start()

    for cv in range(2):
        for which in range(2):
            for ok, row in ((up_ok, 0), (down_ok, R + 1)):
                @pl.when(jnp.logical_not(ok))
                def _():
                    F[cv, 2 * which, row, pl.ds(0, W)] = jnp.zeros((W, CH), jnp.bfloat16)

                for side, across in ((0, left_ok), (1, right_ok)):
                    @pl.when(jnp.logical_not(jnp.logical_and(ok, across)))
                    def _():
                        L[cv, which, side, row] = jnp.zeros((EDGE, CH), jnp.bfloat16)
            for side, across in ((0, left_ok), (1, right_ok)):
                @pl.when(jnp.logical_not(across))
                def _():
                    L[cv, which, side, pl.ds(1, R)] = jnp.zeros((R, EDGE, CH), jnp.bfloat16)

    for cp in [lat_cp, pw_cp] + bias_cp:
        cp.wait()

    def project(i, carry):
        v = jnp.dot(lat[i], pw[...], preferred_element_type=jnp.float32) + pb[...]
        v = v.astype(jnp.bfloat16).astype(jnp.float32)
        a = v / (1.0 + jnp.exp(-v))
        ca[i] = a.astype(jnp.bfloat16)
        for k in range(2):
            s1[pl.ds(k, HW, stride=2), :] = v
            s2[pl.ds(k, HW, stride=2), :] = a
        up[i] = s1[...].astype(jnp.bfloat16)
        wide = s2[...].astype(jnp.bfloat16)
        F[0, 2, 1 + 2 * i, pl.ds(0, W)] = wide
        F[0, 2, 2 + 2 * i, pl.ds(0, W)] = wide
        return carry

    lax.fori_loop(0, HR, project, 0)
    send_sides(0, 1, range(8))

    @pl.when(f == 0)
    def _():
        for i in range(blocks):
            main_copy(0, i, False).start()

    send_sides(1, 0, range(8), True)

    @pl.when(f == 1)
    def _():
        for i in range(blocks):
            main_copy(1, i, True).start()

    def weights(cv, frames):
        return jnp.concatenate([w[cv, a].reshape(3 * CH, 3 * CH) for a in frames], axis=0)

    def taps(cv, frames, i, size):
        lhs = jnp.concatenate(
            [F[cv, a, pl.ds(i + p, size)].reshape(size * W, CH)
             for a in frames for p in range(3)], axis=1)
        return jnp.dot(lhs, weights(cv, frames), preferred_element_type=jnp.float32)

    spot = lax.broadcasted_iota(jnp.int32, (8, CH), 0)

    def fold(z, n):
        z = z[n * W:(n + 1) * W]
        after = pltpu.roll(z[:, :CH], 1, 0)
        after = jnp.concatenate([jnp.where(spot == 0, 0.0, after[:8]), after[8:]], axis=0)
        ahead = pltpu.roll(z[:, 2 * CH:], W - 1, 0)
        ahead = jnp.concatenate([ahead[:W - 8], jnp.where(spot == 7, 0.0, ahead[W - 8:])], axis=0)
        return after + z[:, CH:2 * CH] + ahead

    def begin(cv, frames, size=1):
        def body(i):
            z = taps(cv, frames, i, size)
            for n in range(size):
                acc[i + n] = fold(z, n)
        return body

    def more(cv, frames, size=1):
        def body(i):
            z = taps(cv, frames, i, size)
            for n in range(size):
                acc[i + n] += fold(z, n)
        return body

    def sides(cv):
        lhs = jnp.concatenate(
            [S[cv, a, pl.ds(p, R)].reshape(R * EDGE, CH) for a in range(3) for p in range(3)],
            axis=1)
        z = jnp.dot(lhs, weights(cv, range(3)), preferred_element_type=jnp.float32)
        for n in range(R):
            part = z[n * EDGE:(n + 1) * EDGE]
            acc[n, pl.ds(0, 1)] += part[EDGE - 1:, :CH]
            acc[n, pl.ds(W - 1, 1)] += part[:1, 2 * CH:]

    def finish_one(i):
        for n in range(STEP):
            y = acc[i * STEP + n] + b1[...]
            F[1, 2, i * STEP + n + 1] = (y / (1.0 + jnp.exp(-y))).astype(jnp.bfloat16)

        @pl.when(f == 0)
        def _():
            main_copy(1, i, False).start()

    def out_copy(i):
        here = pl.ds(i * STEP, STEP)
        return pltpu.make_async_copy(obuf.at[here], out_h.at[0, here], out_sem.at[i])

    def finish_two(i):
        base = i * STEP
        for n in range(STEP):
            y = acc[base + n] + b2[...] + up[(base + n) // 2].astype(jnp.float32)
            obuf[base + n] = y.astype(jnp.bfloat16)
        out_copy(i).start()

    def each(body, start, count):
        def step(k, carry):
            body(lax.rem(start + k, blocks))
            return carry

        lax.fori_loop(0, count, step, 0)

    def inner(body):
        each(body, 1, blocks - 2)

    group = max(n for n in (1, 2, GROUP) if (R - 2) % n == 0)

    def inner_dots(make, cv, frames):
        body = make(cv, frames, group)

        def step(k, carry):
            body(1 + k * group)
            return carry

        lax.fori_loop(0, (R - 2) // group, step, 0)

    def outer(body):
        each(body, blocks - 1, 2)

    cols, tall_ds = (2, 3), (0, 1, 4, 5, 6, 7)

    def mids(cv):
        for i in range(blocks):
            main_copy(cv, i, False).wait_recv()

    cache_cp[0].wait()
    for cp in w_cp[0]:
        cp.wait()
    inner_dots(begin, 0, (0, 2))
    mids(0)
    inner_dots(more, 0, (1,))
    recv_sides(0, 0, range(8))
    merge(0, 0)

    @pl.when(f == 1)
    def _():
        for part in range(3):
            rim_copy(0, part).start()

    recv_sides(0, 1, range(8))
    merge(0, 1)
    for k, ok in ((0, up_ok), (1, down_ok)):
        @pl.when(ok)
        def _():
            a = CL[k].astype(jnp.float32)
            for n in range(2):
                s2[pl.ds(n, HW, stride=2), :] = a
            F[0, 2, k * (R + 1)] = s2[...].astype(jnp.bfloat16)

    @pl.when(f == 0)
    def _():
        for part in range(3):
            rim_copy(0, part).start()

    outer(begin(0, (0, 2)))
    for part in range(3):
        rim_copy(0, part).wait_recv()
    outer(more(0, (1,)))
    sides(0)
    outer(finish_one)
    send_sides(1, 1, tall_ds)
    inner(finish_one)
    send_sides(1, 1, cols)

    cache_cp[1].wait()
    for cp in w_cp[1]:
        cp.wait()
    recv_sides(1, 0, range(8))
    merge(1, 0)

    @pl.when(f == 1)
    def _():
        for part in range(3):
            rim_copy(1, part).start()

    inner_dots(begin, 1, (0,))
    outer(begin(1, (0,)))
    mids(1)
    inner_dots(more, 1, (1, 2))
    recv_sides(1, 1, range(8))
    merge(1, 1)

    @pl.when(f == 0)
    def _():
        for part in range(3):
            rim_copy(1, part).start()

    outer(more(1, (2,)))
    for part in range(3):
        rim_copy(1, part).wait_recv()
    sides(1)
    inner(finish_two)
    outer(more(1, (1,)))
    outer(finish_two)

    for cv in range(2):
        for which in range(2):
            drain_sides(cv, which)
        for i in range(blocks):
            main_copy(cv, i, False).wait_send()
        for part in range(3):
            rim_copy(cv, part).wait_send()
    for i in range(blocks):
        out_copy(i).wait()


def per_device(latent, proj_weight, proj_bias, cache_one, cache_two,
               conv_one, bias_one, conv_two, bias_two):
    _, R, W, CH = cache_one.shape
    _, HR, HW, LCH = latent.shape
    blocks = R // STEP
    anywhere = pl.BlockSpec(memory_space=pl.ANY)
    bf = jnp.bfloat16
    return pl.pallas_call(
        functools.partial(kernel, lax.axis_size("row"), lax.axis_size("col")),
        out_shape=jax.ShapeDtypeStruct(cache_one.shape, bf),
        in_specs=[anywhere] * 9,
        out_specs=anywhere,
        scratch_shapes=[
            pltpu.VMEM((HR, HW, LCH), bf),
            pltpu.VMEM((LCH, CH), bf),
            pltpu.VMEM((2, 3, 3, CH, 3 * CH), bf),
            pltpu.VMEM((2, 3, R + 2, W, CH), bf),
            pltpu.VMEM((2, 3, R + 2, EDGE, CH), bf),
            pltpu.VMEM((2, 2, 2, R + 2, EDGE, CH), bf),
            pltpu.VMEM((HR, W, CH), bf),
            pltpu.VMEM((R, W, CH), bf),
            pltpu.VMEM((R, W, CH), jnp.float32),
            pltpu.VMEM((HR, HW, CH), bf),
            pltpu.VMEM((2, HW, CH), bf),
            pltpu.VMEM((W, CH), jnp.float32),
            pltpu.VMEM((W, CH), jnp.float32),
            pltpu.VMEM((1, CH), jnp.float32),
            pltpu.VMEM((1, CH), jnp.float32),
            pltpu.VMEM((1, CH), jnp.float32),
            pltpu.SemaphoreType.DMA((13,)),
            pltpu.SemaphoreType.DMA((2, 2, 8)),
            pltpu.SemaphoreType.DMA((2, 2, 8)),
            pltpu.SemaphoreType.DMA((2, blocks + 3)),
            pltpu.SemaphoreType.DMA((2, blocks + 3)),
            pltpu.SemaphoreType.DMA((blocks,)),
        ],
        compiler_params=pltpu.CompilerParams(
            collective_id=0, has_side_effects=True, vmem_limit_bytes=60 * 1024 * 1024),
        name="decoder_window",
    )(latent, proj_weight, proj_bias.reshape(1, CH), cache_one, cache_two,
      conv_one, bias_one.reshape(1, CH), conv_two, bias_two.reshape(1, CH))


def solution(mesh):
    placed = P(("grp", "frm"), "row", "col", None)
    return jax.shard_map(
        per_device,
        mesh=mesh,
        in_specs=(placed, P(), P(), placed, placed, P(), P(), P(), P()),
        out_specs=placed,
        check_vma=False,
    )
```

```python
import functools

import jax
import jax.numpy as jnp
from jax import lax
from jax.experimental import pallas as pl
from jax.experimental.pallas import tpu as pltpu
from jax.sharding import PartitionSpec as P

EDGE = 16
STEP = 1
GROUP = 2
MESH = pl.DeviceIdType.MESH
SIDES = [(-1, 0), (1, 0), (0, -1), (0, 1), (-1, -1), (-1, 1), (1, -1), (1, 1)]


def kernel(rows_n, cols_n, lat_h, pw_h, pb_h, c1_h, c2_h, w1_h, b1_h, w2_h, b2_h, out_h,

           lat, pw, w, F, S, L, up, obuf, acc, ca, CL, s1, s2, pb, b1, b2,
           load_sem, send_sem, recv_sem, mid_send, mid_recv, out_sem):
    R, W = c1_h.shape[1], c1_h.shape[2]
    CH = c1_h.shape[3]
    HR, HW = lat.shape[0], lat.shape[1]
    blocks = R // STEP
    r, c, f = lax.axis_index("row"), lax.axis_index("col"), lax.axis_index("frm")
    caches = (c1_h, c2_h)
    up_ok, down_ok = r > 0, r < rows_n - 1
    left_ok, right_ok = c > 0, c < cols_n - 1

    def exists(d):
        dr, dc = SIDES[d]
        ok = None
        for test in ([up_ok] if dr < 0 else [down_ok] if dr > 0 else []) + (
                [left_ok] if dc < 0 else [right_ok] if dc > 0 else []):
            ok = test if ok is None else jnp.logical_and(ok, test)
        return ok

    def where_is(d):
        dr, dc = SIDES[d]
        ids = {}
        if dr:
            ids["row"] = r + dr
        if dc:
            ids["col"] = c + dc
        return ids

    loads = []

    def load(src, dst):
        cp = pltpu.make_async_copy(src, dst, load_sem.at[len(loads)])
        cp.start()
        loads.append(cp)
        return cp

    lat_cp = load(lat_h.at[0], lat)
    pw_cp = load(pw_h, pw)
    bias_cp = [load(src, dst) for src, dst in ((pb_h, pb), (b1_h, b1), (b2_h, b2))]
    cache_cp = [load(caches[0].at[0], F.at[0, 0, pl.ds(1, R), pl.ds(0, W)])]
    w_cp = [[load(w1_h.at[:, :, q], w.at[0, :, :, :, pl.ds(q * CH, CH)]) for q in range(3)]]
    cache_cp.append(load(caches[1].at[0], F.at[1, 0, pl.ds(1, R), pl.ds(0, W)]))
    w_cp.append([load(w2_h.at[:, :, q], w.at[1, :, :, :, pl.ds(q * CH, CH)]) for q in range(3)])

    barrier = pltpu.get_barrier_semaphore()
    for d in range(8):
        @pl.when(exists(d))
        def _():
            pl.semaphore_signal(barrier, inc=1, device_id=where_is(d), device_id_type=MESH)
    pl.semaphore_signal(barrier, inc=1, device_id={"frm": 1 - f}, device_id_type=MESH)
    for cv in range(2):
        for which in range(2):
            for ok, row in ((up_ok, 0), (down_ok, R + 1)):
                @pl.when(jnp.logical_not(ok))
                def _():
                    F[cv, 2 * which, row, pl.ds(0, W)] = jnp.zeros((W, CH), jnp.bfloat16)

                for side, across in ((0, left_ok), (1, right_ok)):
                    @pl.when(jnp.logical_not(jnp.logical_and(ok, across)))
                    def _():
                        L[cv, which, side, row] = jnp.zeros((EDGE, CH), jnp.bfloat16)
            for side, across in ((0, left_ok), (1, right_ok)):
                @pl.when(jnp.logical_not(across))
                def _():
                    L[cv, which, side, pl.ds(1, R)] = jnp.zeros((R, EDGE, CH), jnp.bfloat16)

    tall = 1 + up_ok.astype(jnp.int32) + down_ok.astype(jnp.int32)
    wide = 1 + left_ok.astype(jnp.int32) + right_ok.astype(jnp.int32)
    pl.semaphore_wait(barrier, tall * wide)

    def side_copy(cv, which, d, from_hbm=False):
        dr, dc = SIDES[d]
        row = 0 if dr < 0 else R - 1
        land_row = R + 1 if dr < 0 else 0
        col = pl.ds(0, EDGE) if dc < 0 else pl.ds(W - EDGE, EDGE)
        side = 1 if dc < 0 else 0
        fr = 2 * which
        if dc == 0:
            rs, cs = pl.ds(row, 1), pl.ds(0, W)
            dst = F.at[cv, fr, pl.ds(land_row, 1), pl.ds(0, W)]
        elif dr == 0:
            rs, cs = pl.ds(0, R), col
            dst = L.at[cv, which, side, pl.ds(1, R)]
        else:
            rs, cs = pl.ds(row, 1), col
            dst = L.at[cv, which, side, pl.ds(land_row, 1)]
        if cv == 0 and which == 1 and dc == 0:
            src = ca.at[pl.ds(0 if dr < 0 else HR - 1, 1)]
            dst = CL.at[pl.ds(1 if dr < 0 else 0, 1)]
        elif from_hbm:
            src = caches[cv].at[0, rs, cs]
        else:
            src = F.at[cv, fr, pl.ds(1 + rs.start, rs.size), cs]
        return pltpu.make_async_remote_copy(
            src_ref=src, dst_ref=dst, send_sem=send_sem.at[cv, which, d],
            recv_sem=recv_sem.at[cv, which, d], device_id=where_is(d), device_id_type=MESH)

    def send_sides(cv, which, ds, from_hbm=False):
        for d in ds:
            @pl.when(exists(d))
            def _():
                side_copy(cv, which, d, from_hbm).start()

    def recv_sides(cv, which, ds):
        for d in ds:
            opposite = SIDES.index((-SIDES[d][0], -SIDES[d][1]))

            @pl.when(exists(opposite))
            def _():
                side_copy(cv, which, d, which == 0).wait_recv()

    def drain_sides(cv, which):
        for d in range(8):
            @pl.when(exists(d))
            def _():
                side_copy(cv, which, d, which == 0).wait_send()

    partner = {"frm": 1 - f}

    def main_copy(cv, i, cache):
        here = pl.ds(1 + i * STEP, STEP)
        if cache:
            src = caches[cv].at[0, pl.ds(i * STEP, STEP)]
        else:
            src = F.at[cv, 2, here, pl.ds(0, W)]
        return pltpu.make_async_remote_copy(
            src_ref=src, dst_ref=F.at[cv, 1, here, pl.ds(0, W)], send_sem=mid_send.at[cv, i],
            recv_sem=mid_recv.at[cv, i], device_id=partner, device_id_type=MESH)

    payload = 2 * (1 - f)

    def rim_copy(cv, part):
        if part < 2:
            src, dst = (F.at[cv, fr, pl.ds((R + 1) * part, 1)] for fr in (payload, 1))
        else:
            src, dst = (S.at[cv, fr] for fr in (payload, 1))
        return pltpu.make_async_remote_copy(
            src_ref=src, dst_ref=dst,
            send_sem=mid_send.at[cv, blocks + part], recv_sem=mid_recv.at[cv, blocks + part],
            device_id=partner, device_id_type=MESH)

    def merge(cv, which):
        left, right = L[cv, which, 0], L[cv, which, 1]
        place = lax.broadcasted_iota(jnp.int32, left.shape, 1)
        tile = jnp.where(place < EDGE // 2, right.astype(jnp.float32), left.astype(jnp.float32))
        S[cv, 2 * which] = tile.astype(jnp.bfloat16)

    send_sides(0, 0, range(8), True)

    @pl.when(f == 1)
    def _():
        for i in range(blocks):
            main_copy(0, i, True).start()

    for cp in [lat_cp, pw_cp] + bias_cp:
        cp.wait()

    def project(i, carry):
        v = jnp.dot(lat[i], pw[...], preferred_element_type=jnp.float32) + pb[...]
        v = v.astype(jnp.bfloat16).astype(jnp.float32)
        a = v / (1.0 + jnp.exp(-v))
        ca[i] = a.astype(jnp.bfloat16)
        for k in range(2):
            s1[pl.ds(k, HW, stride=2), :] = v
            s2[pl.ds(k, HW, stride=2), :] = a
        up[i] = s1[...].astype(jnp.bfloat16)
        wide = s2[...].astype(jnp.bfloat16)
        F[0, 2, 1 + 2 * i, pl.ds(0, W)] = wide
        F[0, 2, 2 + 2 * i, pl.ds(0, W)] = wide
        return carry

    lax.fori_loop(0, HR, project, 0)
    send_sides(0, 1, range(8))

    @pl.when(f == 0)
    def _():
        for i in range(blocks):
            main_copy(0, i, False).start()

    send_sides(1, 0, range(8), True)

    @pl.when(f == 1)
    def _():
        for i in range(blocks):
            main_copy(1, i, True).start()

    def weights(cv, frames):
        return jnp.concatenate([w[cv, a].reshape(3 * CH, 3 * CH) for a in frames], axis=0)

    def taps(cv, frames, i, size):
        lhs = jnp.concatenate(
            [F[cv, a, pl.ds(i + p, size)].reshape(size * W, CH)
             for a in frames for p in range(3)], axis=1)
        return jnp.dot(lhs, weights(cv, frames), preferred_element_type=jnp.float32)

    spot = lax.broadcasted_iota(jnp.int32, (8, CH), 0)

    def fold(z, n):
        z = z[n * W:(n + 1) * W]
        after = pltpu.roll(z[:, :CH], 1, 0)
        after = jnp.concatenate([jnp.where(spot == 0, 0.0, after[:8]), after[8:]], axis=0)
        ahead = pltpu.roll(z[:, 2 * CH:], W - 1, 0)
        ahead = jnp.concatenate([ahead[:W - 8], jnp.where(spot == 7, 0.0, ahead[W - 8:])], axis=0)
        return after + z[:, CH:2 * CH] + ahead

    def begin(cv, frames, size=1):
        def body(i):
            z = taps(cv, frames, i, size)
            for n in range(size):
                acc[i + n] = fold(z, n)
        return body

    def more(cv, frames, size=1):
        def body(i):
            z = taps(cv, frames, i, size)
            for n in range(size):
                acc[i + n] += fold(z, n)
        return body

    def sides(cv):
        lhs = jnp.concatenate(
            [S[cv, a, pl.ds(p, R)].reshape(R * EDGE, CH) for a in range(3) for p in range(3)],
            axis=1)
        z = jnp.dot(lhs, weights(cv, range(3)), preferred_element_type=jnp.float32)
        for n in range(R):
            part = z[n * EDGE:(n + 1) * EDGE]
            acc[n, pl.ds(0, 1)] += part[EDGE - 1:, :CH]
            acc[n, pl.ds(W - 1, 1)] += part[:1, 2 * CH:]

    def finish_one(i):
        for n in range(STEP):
            y = acc[i * STEP + n] + b1[...]
            F[1, 2, i * STEP + n + 1] = (y / (1.0 + jnp.exp(-y))).astype(jnp.bfloat16)

        @pl.when(f == 0)
        def _():
            main_copy(1, i, False).start()

    def out_copy(i):
        here = pl.ds(i * STEP, STEP)
        return pltpu.make_async_copy(obuf.at[here], out_h.at[0, here], out_sem.at[i])

    def finish_two(i):
        base = i * STEP
        for n in range(STEP):
            y = acc[base + n] + b2[...] + up[(base + n) // 2].astype(jnp.float32)
            obuf[base + n] = y.astype(jnp.bfloat16)
        out_copy(i).start()

    def each(body, start, count):
        def step(k, carry):
            body(lax.rem(start + k, blocks))
            return carry

        lax.fori_loop(0, count, step, 0)

    def inner(body):
        each(body, 1, blocks - 2)

    group = max(n for n in (1, 2, GROUP) if (R - 2) % n == 0)

    def inner_dots(make, cv, frames):
        body = make(cv, frames, group)

        def step(k, carry):
            body(1 + k * group)
            return carry

        lax.fori_loop(0, (R - 2) // group, step, 0)

    def outer(body):
        each(body, blocks - 1, 2)

    cols, tall_ds = (2, 3), (0, 1, 4, 5, 6, 7)

    def mids(cv):
        for i in range(blocks):
            main_copy(cv, i, False).wait_recv()

    cache_cp[0].wait()
    for cp in w_cp[0]:
        cp.wait()
    inner_dots(begin, 0, (0, 2))
    mids(0)
    inner_dots(more, 0, (1,))
    recv_sides(0, 0, range(8))
    merge(0, 0)

    @pl.when(f == 1)
    def _():
        for part in range(3):
            rim_copy(0, part).start()

    recv_sides(0, 1, range(8))
    merge(0, 1)
    for k, ok in ((0, up_ok), (1, down_ok)):
        @pl.when(ok)
        def _():
            a = CL[k].astype(jnp.float32)
            for n in range(2):
                s2[pl.ds(n, HW, stride=2), :] = a
            F[0, 2, k * (R + 1)] = s2[...].astype(jnp.bfloat16)

    @pl.when(f == 0)
    def _():
        for part in range(3):
            rim_copy(0, part).start()

    outer(begin(0, (0, 2)))
    for part in range(3):
        rim_copy(0, part).wait_recv()
    outer(more(0, (1,)))
    sides(0)
    outer(finish_one)
    send_sides(1, 1, tall_ds)
    inner(finish_one)
    send_sides(1, 1, cols)

    cache_cp[1].wait()
    for cp in w_cp[1]:
        cp.wait()
    recv_sides(1, 0, range(8))
    merge(1, 0)

    @pl.when(f == 1)
    def _():
        for part in range(3):
            rim_copy(1, part).start()

    inner_dots(begin, 1, (0,))
    outer(begin(1, (0,)))
    mids(1)
    inner_dots(more, 1, (1, 2))
    recv_sides(1, 1, range(8))
    merge(1, 1)

    @pl.when(f == 0)
    def _():
        for part in range(3):
            rim_copy(1, part).start()

    outer(more(1, (2,)))
    for part in range(3):
        rim_copy(1, part).wait_recv()
    sides(1)
    inner(finish_two)
    outer(more(1, (1,)))
    outer(finish_two)

    for cv in range(2):
        for which in range(2):
            drain_sides(cv, which)
        for i in range(blocks):
            main_copy(cv, i, False).wait_send()
        for part in range(3):
            rim_copy(cv, part).wait_send()
    for i in range(blocks):
        out_copy(i).wait()


def per_device(latent, proj_weight, proj_bias, cache_one, cache_two,
               conv_one, bias_one, conv_two, bias_two):
    _, R, W, CH = cache_one.shape
    _, HR, HW, LCH = latent.shape
    blocks = R // STEP
    anywhere = pl.BlockSpec(memory_space=pl.ANY)
    bf = jnp.bfloat16
    return pl.pallas_call(
        functools.partial(kernel, lax.axis_size("row"), lax.axis_size("col")),
        out_shape=jax.ShapeDtypeStruct(cache_one.shape, bf),
        in_specs=[anywhere] * 9,
        out_specs=anywhere,
        scratch_shapes=[
            pltpu.VMEM((HR, HW, LCH), bf),
            pltpu.VMEM((LCH, CH), bf),
            pltpu.VMEM((2, 3, 3, CH, 3 * CH), bf),
            pltpu.VMEM((2, 3, R + 2, W, CH), bf),
            pltpu.VMEM((2, 3, R + 2, EDGE, CH), bf),
            pltpu.VMEM((2, 2, 2, R + 2, EDGE, CH), bf),
            pltpu.VMEM((HR, W, CH), bf),
            pltpu.VMEM((R, W, CH), bf),
            pltpu.VMEM((R, W, CH), jnp.float32),
            pltpu.VMEM((HR, HW, CH), bf),
            pltpu.VMEM((2, HW, CH), bf),
            pltpu.VMEM((W, CH), jnp.float32),
            pltpu.VMEM((W, CH), jnp.float32),
            pltpu.VMEM((1, CH), jnp.float32),
            pltpu.VMEM((1, CH), jnp.float32),
            pltpu.VMEM((1, CH), jnp.float32),
            pltpu.SemaphoreType.DMA((13,)),
            pltpu.SemaphoreType.DMA((2, 2, 8)),
            pltpu.SemaphoreType.DMA((2, 2, 8)),
            pltpu.SemaphoreType.DMA((2, blocks + 3)),
            pltpu.SemaphoreType.DMA((2, blocks + 3)),
            pltpu.SemaphoreType.DMA((blocks,)),
        ],
        compiler_params=pltpu.CompilerParams(
            collective_id=0, has_side_effects=True, vmem_limit_bytes=60 * 1024 * 1024),
        name="decoder_window",
    )(latent, proj_weight, proj_bias.reshape(1, CH), cache_one, cache_two,
      conv_one, bias_one.reshape(1, CH), conv_two, bias_two.reshape(1, CH))


def solution(mesh):
    placed = P(("grp", "frm"), "row", "col", None)
    return jax.shard_map(
        per_device,
        mesh=mesh,
        in_specs=(placed, P(), P(), placed, placed, P(), P(), P(), P()),
        out_specs=placed,
        check_vma=False,
    )
```
